512 devices in a mesh: dp: 2 (over core), pipe: 4 (over x), ctx: 64 (over z, y).
Axes of the slice: x: 4, y: 8, z: 8, core: 2. Of those that a mesh axis runs over, the one named last changes fastest.
Arguments:
- inputs: bfloat16 [4, 4096, 768], P('dp', 'ctx'), may hold values from -16 to 16
- cotangent: bfloat16 [4, 4096, 768], P('dp', 'ctx'), may hold values from -6 to 6
- dilated_kernel_weight: bfloat16 [4, 3, 768, 384], P('pipe'), may hold values from -0.125 to 0.125
- point_weight: bfloat16 [4, 384, 768], P('pipe'), may hold values from -0.3125 to 0.3125
Outputs:
- dilated_grad: float32 [4, 3, 768, 384], P('pipe', None, ('dp', 'ctx'))
The draws below stay inside these ranges and needn't reach their ends.
All inputs are finite; a program needn't handle non-finite values.
Results may differ from the reference program's by a relative error of at most 0.012.
Values may be sent and summed in bfloat16 or wider, within the bound.
A program may use at most 64 MiB of HBM per device.

```python
import math
import jax
import jax.numpy as jnp
from jax import lax

C = 768
B = 384
BIN_DEV = 64
NBINS = 4096
SEQS = 4
N_PIPE = 4


def spiked(result, rng, source, target, blocks, factor):
    def block_of(position):
        return (jnp.arange(result.shape[position]) // (result.shape[position] // blocks)).reshape((-1,) + (1,) * (result.ndim - 1 - position))

    first = jax.random.permutation(rng, blocks)[block_of(target)]
    other_side = (block_of(target) + blocks // 2) % blocks
    return jnp.where((block_of(source) == first) | (block_of(source) == other_side), factor * result, result)


def block_levels(key, dims, split, low, largest):
    loudness = 1.0
    for axis_at, parts in split:
        draws = jax.random.uniform(jax.random.fold_in(jax.random.fold_in(key, 6), axis_at), (parts,), jnp.float32, low / len(split), largest / len(split))
        loudness = loudness * jnp.repeat(jnp.exp(draws), dims[axis_at] // parts).reshape((-1,) + (1,) * (len(dims) - 1 - axis_at))
    return loudness


def scatter_about(stream_key, extent, scale, most, pieces=(), kind=jnp.bfloat16):
    result = scale * jax.random.normal(stream_key, extent, jnp.float32)
    if pieces:
        result = result * block_levels(stream_key, extent, pieces, -0.22, 0.18)
    return jnp.clip(result, -most, most).astype(kind)


def gaussian_with(key, dims, scale, bound, cuts, heavy, dtype=jnp.bfloat16):
    result = scale * jax.random.normal(key, dims, jnp.float32)
    if cuts:
        result = result * block_levels(key, dims, cuts, -0.22, 0.18)
    return jnp.clip(spiked(result, jax.random.fold_in(key, 3), *heavy), -bound, bound).astype(dtype)


def setup_inputs(seed: int = 0) -> dict:
    arg_keys = jax.random.split(jax.random.key(seed), 5)
    inputs = gaussian_with(arg_keys[0], (SEQS, NBINS, C), 1.0, 16.0, ((0, 2), (1, 64)), (1, 2, 64, 4.0))
    cotangent = scatter_about(arg_keys[1], (SEQS, NBINS, C), 1.0, 6.0, ((0, 2), (1, 64)))
    dilated_kernel_weight = scatter_about(arg_keys[2], (N_PIPE, 3, C, B), (3 * C) ** -0.5, 0.125, ((0, 4),))
    point_weight = scatter_about(arg_keys[3], (N_PIPE, B, C), B ** -0.5, 0.3125, ((0, 4),))
    return {"inputs": inputs, "cotangent": cotangent, "dilated_kernel_weight": dilated_kernel_weight, "point_weight": point_weight}


root_half = 0.7071067811865476
inv_root_two_pi = 0.3989422804014327

def gelu(value):
    return 0.5 * value * (1.0 + lax.erf(value * root_half))

def gelu_slope(value):
    return 0.5 * (1.0 + lax.erf(value * root_half)) + value * jnp.exp(-0.5 * value * value) * inv_root_two_pi

def reference(inputs, cotangent, dilated_kernel_weight, point_weight):
    layers = N_PIPE
    reach = BIN_DEV // 2
    length = NBINS
    scale = 1.0 / math.sqrt(SEQS * NBINS)
    trunk = inputs
    saved = []
    for layer in range(layers):
        spread = reach // 2 ** (layers - 1 - layer)
        act = gelu(trunk.astype(jnp.float32)).astype(jnp.bfloat16)
        padded = jnp.pad(act, ((0, 0), (spread, spread), (0, 0)))
        pre = jnp.zeros(act.shape[:2] + (dilated_kernel_weight.shape[3],), jnp.float32)
        for kernel_offset in range(3):
            receptive_span = padded[:, kernel_offset * spread:kernel_offset * spread + length]
            pre = pre + jnp.dot(receptive_span, dilated_kernel_weight[layer, kernel_offset], preferred_element_type=jnp.float32)
        inner = gelu(pre).astype(jnp.bfloat16)
        branch = jnp.dot(inner, point_weight[layer], preferred_element_type=jnp.float32)
        saved.append((trunk, padded, pre))
        trunk = (trunk.astype(jnp.float32) + branch).astype(jnp.bfloat16)
    upstream = (cotangent.astype(jnp.float32) * scale).astype(jnp.bfloat16)
    grads = [None] * layers
    for layer in reversed(range(layers)):
        spread = reach // 2 ** (layers - 1 - layer)
        trunk_in, padded, pre = saved[layer]
        inner_grad = jnp.dot(upstream, point_weight[layer].T, preferred_element_type=jnp.float32)
        dpre = (inner_grad * gelu_slope(pre)).astype(jnp.bfloat16)
        dpre_wide = dpre.astype(jnp.float32)
        taps = []
        for kernel_offset in range(3):
            receptive_span = padded[:, kernel_offset * spread:kernel_offset * spread + length].astype(jnp.float32)
            taps.append(jnp.einsum('snc,snb->cb', receptive_span, dpre_wide))
        grads[layer] = jnp.stack(taps)
        dpad = jnp.pad(dpre, ((0, 0), (spread, spread), (0, 0)))
        dact = jnp.zeros(trunk_in.shape, jnp.float32)
        for kernel_offset in range(3):
            receptive_span = dpad[:, (2 - kernel_offset) * spread:(2 - kernel_offset) * spread + length]
            dact = dact + jnp.dot(receptive_span, dilated_kernel_weight[layer, kernel_offset].T, preferred_element_type=jnp.float32)
        upstream = (upstream.astype(jnp.float32) + dact * gelu_slope(trunk_in.astype(jnp.float32))).astype(jnp.bfloat16)
    return jnp.stack(grads)
```

```python
import math

import jax
import jax.numpy as jnp
from jax import lax
from jax.experimental import pallas as pl
from jax.experimental.pallas import tpu as pltpu
from jax.sharding import PartitionSpec as P

MESH = pl.DeviceIdType.MESH
F32 = jnp.float32
BF16 = jnp.bfloat16
RING = 8
OWN = 64
LEFT = 128
ROWS = 320
PAD = 16
C = 768
B = 384
WROWS = 3072
QUARTER = 192
root_half = 0.7071067811865476
inv_root_two_pi = 0.3989422804014327
FORE = ((0, 320), (16, 288), (32, 256), (64, 192))
BACK = ((128, 64), (112, 96), (96, 128), (64, 192))
DILATION = (4, 8, 16, 32)


def gelu_and_slope(value):
    bell = jnp.exp(-0.5 * value * value)
    t = 1.0 / (1.0 + (0.3275911 * root_half) * jnp.abs(value))
    series = t * (
        0.127414796 + t * (-0.142248368 + t * (0.7107068705 + t * (-0.7265760135 + t * 0.5307027145)))
    )
    tail = series * bell
    phi = jnp.where(value >= 0.0, 1.0 - tail, tail)
    return value * phi, phi + value * bell * inv_root_two_pi


def remote(src, dst, send, recv, device):
    return pltpu.make_async_remote_copy(
        src_ref=src, dst_ref=dst, send_sem=send, recv_sem=recv, device_id=device, device_id_type=MESH
    )


def meet(devices):
    barrier = pltpu.get_barrier_semaphore()
    for device in devices:
        pl.semaphore_signal(barrier, inc=1, device_id=device, device_id_type=MESH)
    pl.semaphore_wait(barrier, len(devices))


def place():
    core = lax.axis_index("dp")
    pipe = lax.axis_index("pipe")
    ctx = lax.axis_index("ctx")
    return core, pipe, ctx, ctx // RING, ctx % RING


def at(core, pipe, ctx):
    return (core, pipe, ctx)


def on_torus(z, y):
    return ((z + RING) % RING) * RING + (y + RING) % RING


class Copies:
    def __init__(self, send, recv):
        self.send, self.recv, self.made, self.number = send, recv, {}, {}

    def start(self, name, src, dst, device):
        i = self.number.setdefault(name, len(self.number))
        copy = remote(src, dst, self.send.at[i], self.recv.at[i], device)
        copy.start()
        self.made[name] = copy

    def arrived(self, name, dst, device):
        i = self.number[name]
        remote(dst, dst, self.send.at[i], self.recv.at[i], device).wait_recv()

    def drain(self):
        for copy in self.made.values():
            copy.wait_send()


def gather_kernel(inp, cot, wd, wp, wg, xe, ce, local, send, recv):
    core, pipe, ctx, z, y = place()
    count = RING * RING
    ahead, behind = (pipe + 1) % 4, (pipe + 3) % 4
    other = (pipe + 2) % 4
    parity = (y + z) % 2
    near = [on_torus(z + 1, y), on_torus(z - 1, y), on_torus(z, y + 1), on_torus(z, y - 1)]
    partner = at(1 - core, pipe, ctx)
    up, down = at(core, ahead, ctx), at(core, behind, ctx)
    beside = [at(core, pipe, n) for n in near]
    side = {o: at(core, pipe, (ctx + o + count) % count) for o in (1, -1, 2, -2)}

    loads = [pltpu.make_async_copy(wd.at[0, k], wg.at[pipe, pl.ds(k * C, C), :], local.at[k]) for k in range(3)]
    for h in range(2):
        loads.append(
            pltpu.make_async_copy(
                wp.at[0, :, pl.ds(h * B, B)], wg.at[pipe, pl.ds(3 * C + h * B, B), :], local.at[3 + h]
            )
        )
    loads.append(pltpu.make_async_copy(inp, xe.at[:, pl.ds(LEFT, OWN), :], local.at[5]))
    loads.append(pltpu.make_async_copy(cot, ce.at[:, pl.ds(OWN, OWN), :], local.at[6]))
    for load in loads:
        load.start()
    meet([partner, up, down] + beside + list(side.values()))
    for load in loads:
        load.wait()

    mine = (core * 2 + parity) * (4 * QUARTER)
    theirs = (core * 2 + 1 - parity) * (4 * QUARTER)

    def piece(layer, base, n):
        return wg.at[layer, pl.ds(pl.multiple_of(base + n * QUARTER, QUARTER), QUARTER), :]

    copies = Copies(send, recv)
    for n in range(4):
        copies.start(("up", n), piece(pipe, mine, n), piece(pipe, mine, n), up)
        copies.start(("down", n), piece(pipe, mine, n), piece(pipe, mine, n), down)
    copies.start("i+1", inp, xe.at[:, pl.ds(OWN, OWN), :], side[1])
    copies.start("i-1", inp, xe.at[:, pl.ds(LEFT + OWN, OWN), :], side[-1])
    copies.start("c+1", cot.at[:, pl.ds(8, 56), :], ce.at[:, pl.ds(8, 56), :], side[1])
    copies.start("c-1", cot.at[:, pl.ds(0, 56), :], ce.at[:, pl.ds(2 * OWN, 56), :], side[-1])
    copies.start("i+2", inp.at[:, pl.ds(8, 56), :], xe.at[:, pl.ds(8, 56), :], side[2])
    copies.start("i-2", inp.at[:, pl.ds(0, 56), :], xe.at[:, pl.ds(4 * OWN, 56), :], side[-2])

    def spread(layer, tag, n):
        block = piece(layer, mine, n)
        copies.start((tag, "near", n), block, block, beside[n])
        copies.start((tag, "chip", n), block, block, partner)

    for n in range(4):
        copies.arrived(("up", n), piece(behind, mine, n), down)
        if n < 2:
            copies.start(("up2", n), piece(behind, mine, n), piece(behind, mine, n), up)
        spread(behind, "behind", n)
        copies.arrived(("down", n), piece(ahead, mine, n), up)
        if n >= 2:
            copies.start(("down2", n), piece(ahead, mine, n), piece(ahead, mine, n), down)
        spread(ahead, "ahead", n)
    for n in range(4):
        if n < 2:
            copies.arrived(("up2", n), piece(other, mine, n), down)
        else:
            copies.arrived(("down2", n), piece(other, mine, n), up)
        spread(other, "other", n)
    layers = (("behind", behind), ("ahead", ahead), ("other", other))
    for tag, layer in layers:
        for n in range(4):
            block = piece(layer, theirs, n)
            copies.arrived((tag, "near", n), block, beside[n])
            copies.start((tag, "far", n), block, block, partner)
    core_mine = ((1 - core) * 2 + parity) * (4 * QUARTER)
    core_theirs = ((1 - core) * 2 + 1 - parity) * (4 * QUARTER)
    for tag, layer in layers:
        for n in range(4):
            copies.arrived((tag, "chip", n), piece(layer, core_mine, n), partner)
            copies.arrived((tag, "far", n), piece(layer, core_theirs, n), partner)
    copies.arrived("i+1", xe.at[:, pl.ds(OWN, OWN), :], side[-1])
    copies.arrived("i-1", xe.at[:, pl.ds(LEFT + OWN, OWN), :], side[1])
    copies.arrived("c+1", ce.at[:, pl.ds(8, 56), :], side[-1])
    copies.arrived("c-1", ce.at[:, pl.ds(2 * OWN, 56), :], side[1])
    copies.arrived("i+2", xe.at[:, pl.ds(8, 56), :], side[-2])
    copies.arrived("i-2", xe.at[:, pl.ds(4 * OWN, 56), :], side[2])
    copies.drain()


def blocks(first, count, body):
    if count == 0:
        return

    def step(i, carry):
        for s in range(2):
            body(s, pl.multiple_of(first + i * 16, 16))
        return carry

    lax.fori_loop(0, count // 16, step, 0)


def compute_kernel(wg, xe, ce, act_out, dpre_out, xs, acts, pre, inner, slope_x, slope_pre, dy, dpre):
    pipe = lax.axis_index("pipe")
    ctx = lax.axis_index("ctx")
    last = RING * RING - 1

    def outside(ref, shift, low, high):
        for where, first, end in (
            (ctx == 0, low, LEFT),
            (ctx == 1, low, LEFT - OWN),
            (ctx == last, LEFT + OWN, high),
            (ctx == last - 1, LEFT + 2 * OWN, high),
        ):
            if first < end:

                @pl.when(where)
                def _(first=first, end=end):
                    ref[:, pl.ds(first + shift, end - first), :] = jnp.zeros(
                        (2, end - first, ref.shape[2]), ref.dtype
                    )

    def trunk(layer):
        return xe if layer == 0 else xs.at[layer - 1]

    for layer in range(4):
        first, count = FORE[layer]
        d = DILATION[layer]
        x = trunk(layer)
        act = acts.at[layer]
        low = max(first - 16 * pl.cdiv(d, 16), 0)
        high = min(first + count + 16 * pl.cdiv(d, 16), ROWS)

        def plain(s, row):
            value, _ = gelu_and_slope(x[s, pl.ds(row, 16), :].astype(F32))
            act[s, pl.ds(row + PAD, 16), :] = value.astype(BF16)

        if layer > 0:
            keep, kept = BACK[layer - 1]

            def both(s, row):
                value, slope = gelu_and_slope(x[s, pl.ds(row, 16), :].astype(F32))
                act[s, pl.ds(row + PAD, 16), :] = value.astype(BF16)
                slope_x[layer - 1, s, pl.ds(row - 96, 16), :] = slope

            blocks(low, keep - low, plain)
            blocks(keep, kept, both)
            blocks(keep + kept, high - keep - kept, plain)
        else:
            blocks(low, high - low, plain)
        outside(act, PAD, low, high)

        lhs = jnp.concatenate(
            [
                jnp.concatenate(
                    [act[s, pl.ds(first + PAD + (k - 1) * d, count), :] for s in range(2)], axis=0
                )
                for k in range(3)
            ],
            axis=1,
        )
        total = jnp.dot(lhs, wg[layer, pl.ds(0, 3 * C), :], preferred_element_type=F32)
        for s in range(2):
            pre[s, pl.ds(first, count), :] = total[s * count : (s + 1) * count]

        keep, kept = BACK[layer]

        def inner_plain(s, row):
            value, _ = gelu_and_slope(pre[s, pl.ds(row, 16), :])
            inner[s, pl.ds(row, 16), :] = value.astype(BF16)

        def inner_both(s, row):
            value, slope = gelu_and_slope(pre[s, pl.ds(row, 16), :])
            inner[s, pl.ds(row, 16), :] = value.astype(BF16)
            slope_pre[layer, s, pl.ds(row - 64, 16), :] = slope

        blocks(first, keep - first, inner_plain)
        blocks(keep, kept, inner_both)
        blocks(keep + kept, first + count - keep - kept, inner_plain)
        if layer < 3:
            follow = xs.at[layer]
            left = jnp.concatenate([inner[s, pl.ds(first, count), :] for s in range(2)], axis=0)
            for h in range(2):
                product = jnp.dot(left, wg[layer, pl.ds(3 * C + h * B, B), :], preferred_element_type=F32)
                for s in range(2):
                    old = x[s, pl.ds(first, count), pl.ds(h * B, B)].astype(F32)
                    follow[s, pl.ds(first, count), pl.ds(h * B, B)] = (
                        old + product[s * count : (s + 1) * count]
                    ).astype(BF16)

    scale = 1.0 / math.sqrt(4 * 4096)
    transposed = (((1,), (1,)), ((), ()))
    dy[:, pl.ds(64, 192), :] = (ce[...].astype(F32) * scale).astype(BF16)
    for layer in (3, 2, 1, 0):
        first, count = BACK[layer]
        d = DILATION[layer]
        upstream = jnp.concatenate([dy[s, pl.ds(first, count), :] for s in range(2)], axis=0)
        inner_grad = lax.dot_general(
            upstream[:, :B], wg[layer, pl.ds(3 * C, B), :], transposed, preferred_element_type=F32
        ) + lax.dot_general(
            upstream[:, B:], wg[layer, pl.ds(3 * C + B, B), :], transposed, preferred_element_type=F32
        )
        for s in range(2):
            slope = slope_pre[layer, s, pl.ds(first - 64, count), :]
            dpre[s, pl.ds(first, count), :] = (inner_grad[s * count : (s + 1) * count] * slope).astype(BF16)
        outside(dpre, 0, first, first + count)

        @pl.when(pipe == layer)
        def _():
            for s in range(2):
                dpre_out[pl.ds(s * OWN, OWN), :] = dpre[s, pl.ds(LEFT, OWN), :]
                for k in range(3):
                    act_out[k, pl.ds(s * OWN, OWN), :] = acts[
                        layer, s, pl.ds(LEFT + PAD + (k - 1) * d, OWN), :
                    ]

        if layer > 0:
            first, count = BACK[layer - 1]
            total = None
            for k in range(3):
                left = jnp.concatenate(
                    [dpre[s, pl.ds(first - (k - 1) * d, count), :] for s in range(2)], axis=0
                )
                product = lax.dot_general(
                    left, wg[layer, pl.ds(k * C, C), :], transposed, preferred_element_type=F32
                )
                total = product if total is None else total + product
            for s in range(2):
                slope = slope_x[layer - 1, s, pl.ds(first - 96, count), :]
                old = dy[s, pl.ds(first, count), :].astype(F32)
                dy[s, pl.ds(first, count), :] = (old + total[s * count : (s + 1) * count] * slope).astype(BF16)


def reduce_kernel(act, dpre, out, ract, rdpre, g, zs, zr, gz, ys, yr, send, recv):
    core, pipe, ctx, z, y = place()
    partner = at(1 - core, pipe, ctx)
    up = at(core, pipe, on_torus(z + 1, y))
    down = at(core, pipe, on_torus(z - 1, y))
    row = {o: at(core, pipe, on_torus(z, y + o)) for o in range(1, RING)}
    meet([partner, up, down] + list(row.values()))

    def half(which):
        return pl.ds(pl.multiple_of(which * B, B), B)

    copies = Copies(send, recv)
    copies.start("dpre", dpre, rdpre, partner)
    copies.start("act", act.at[:, :, half(1 - core)], ract, partner)
    over_rows = (((0,), (0,)), ((), ()))
    for k in range(3):
        g[k] = lax.dot_general(act[k, :, half(core)], dpre[...], over_rows, preferred_element_type=F32)
    copies.arrived("dpre", rdpre, partner)
    copies.arrived("act", ract, partner)
    for k in range(3):
        g[k] += lax.dot_general(ract[k], rdpre[...], over_rows, preferred_element_type=F32)

    deep = B // RING

    def part(k, offset):
        target = (z + offset + RING) % RING
        return g[k, pl.ds(pl.multiple_of(target * deep, 16), deep), :]

    routes = [("up", up, down, 0, [4, 3, 2, 1]), ("down", down, up, 4, [-3, -2, -1])]
    for step in range(4):
        for name, device, source, base, offsets in routes:
            if step >= len(offsets):
                continue
            slot = base + step
            for k in range(3):
                value = part(k, offsets[step])
                if step > 0:
                    copies.arrived((name, step - 1, k), zr.at[slot - 1, k], source)
                    value = value + zr[slot - 1, k].astype(F32)
                zs[slot, k] = value.astype(BF16)
                copies.start((name, step, k), zs.at[slot, k], zr.at[slot, k], device)
    for k in range(3):
        copies.arrived(("up", 3, k), zr.at[3, k], down)
        copies.arrived(("down", 2, k), zr.at[6, k], up)
        gz[k] = part(k, 0) + zr[3, k].astype(F32) + zr[6, k].astype(F32)

    small = deep // RING
    for j in range(RING):
        for k in range(3):
            ys[j, k, pl.ds(0, small), :] = gz[k, pl.ds(j * small, small), :]
            ys[j, k, pl.ds(small, 2), :] = jnp.zeros((2, B), F32)
    for o in range(1, RING):
        copies.start(("row", o), ys.at[(y + o) % RING], yr.at[o], row[o])
    total = ys[y]
    for o in range(1, RING):
        copies.arrived(("row", o), yr.at[o], row[RING - o])
        total = total + yr[o]
    out[0] = total[:, :small, :]
    copies.drain()


def shards(inputs, cotangent, dilated_kernel_weight, point_weight):
    vmem = pl.BlockSpec(memory_space=pltpu.VMEM)
    anywhere = pl.BlockSpec(memory_space=pl.ANY)
    limit = 60 * 2**20
    wg, xe, ce = pl.pallas_call(
        gather_kernel,
        name="gather",
        out_shape=(
            jax.ShapeDtypeStruct((4, WROWS, B), BF16),
            jax.ShapeDtypeStruct((2, ROWS, C), BF16),
            jax.ShapeDtypeStruct((2, 3 * OWN, C), BF16),
        ),
        in_specs=[anywhere] * 4,
        out_specs=(vmem,) * 3,
        scratch_shapes=[
            pltpu.SemaphoreType.DMA((7,)),
            pltpu.SemaphoreType.DMA((64,)),
            pltpu.SemaphoreType.DMA((64,)),
        ],
        compiler_params=pltpu.CompilerParams(collective_id=0, has_side_effects=True, vmem_limit_bytes=limit),
    )(inputs, cotangent, dilated_kernel_weight, point_weight)
    act, dpre = pl.pallas_call(
        compute_kernel,
        name="tower",
        out_shape=(
            jax.ShapeDtypeStruct((3, 2 * OWN, C), BF16),
            jax.ShapeDtypeStruct((2 * OWN, B), BF16),
        ),
        in_specs=[vmem] * 3,
        out_specs=(vmem,) * 2,
        scratch_shapes=[
            pltpu.VMEM((3, 2, ROWS, C), BF16),
            pltpu.VMEM((4, 2, ROWS + 2 * PAD, C), BF16),
            pltpu.VMEM((2, ROWS, B), F32),
            pltpu.VMEM((2, ROWS, B), BF16),
            pltpu.VMEM((3, 2, 128, C), F32),
            pltpu.VMEM((4, 2, 192, B), F32),
            pltpu.VMEM((2, ROWS, C), BF16),
            pltpu.VMEM((2, ROWS, B), BF16),
        ],
        compiler_params=pltpu.CompilerParams(vmem_limit_bytes=limit),
    )(wg, xe, ce)
    deep = B // RING
    return pl.pallas_call(
        reduce_kernel,
        name="reduce",
        out_shape=jax.ShapeDtypeStruct((1, 3, deep // RING, B), F32),
        in_specs=[vmem] * 2,
        out_specs=vmem,
        scratch_shapes=[
            pltpu.VMEM((3, 2 * OWN, B), BF16),
            pltpu.VMEM((2 * OWN, B), BF16),
            pltpu.VMEM((3, B, B), F32),
            pltpu.VMEM((7, 3, deep, B), BF16),
            pltpu.VMEM((7, 3, deep, B), BF16),
            pltpu.VMEM((3, deep, B), F32),
            pltpu.VMEM((RING, 3, 8, B), F32),
            pltpu.VMEM((RING, 3, 8, B), F32),
            pltpu.SemaphoreType.DMA((32,)),
            pltpu.SemaphoreType.DMA((32,)),
        ],
        compiler_params=pltpu.CompilerParams(collective_id=1, has_side_effects=True, vmem_limit_bytes=limit),
    )(act, dpre)


def solution(mesh):
    return jax.shard_map(
        shards,
        mesh=mesh,
        in_specs=(
            P("dp", "ctx", None),
            P("dp", "ctx", None),
            P("pipe", None, None, None),
            P("pipe", None, None),
        ),
        out_specs=P("pipe", None, ("dp", "ctx"), None),
        check_vma=False,
    )
```
